128 devices in a mesh: dp: 16 (over y_hi, z, core), tensor: 8 (over x, y_lo).
Axes of the slice: x: 4, y: 4 (y_hi: 2, y_lo: 2; y = y_hi * 2 + y_lo), z: 4, core: 2. Of those that a mesh axis runs over, the one named last changes fastest.
Arguments:
- activations: bfloat16 [16384, 8192], P('dp'), may hold values from -6 to 6
- out_grad: bfloat16 [16384, 28672], P('dp', 'tensor'), may hold values from -0.046875 to 0.046875
- projector: bfloat16 [8192, 512], P(('dp', 'tensor')), may hold values from -0.0625 to 0.0625
- first_moment: float32 [512, 28672], P('dp', 'tensor'), may hold values from -3 to 3
- second_moment: float32 [512, 28672], P('dp', 'tensor'), may hold values from 0.1 to 4
Outputs:
- update: float32 [8192, 28672], P('dp', 'tensor')
- new_first: float32 [512, 28672], P('dp', 'tensor')
- new_second: float32 [512, 28672], P('dp', 'tensor')
The draws below stay inside these ranges and needn't reach their ends.
All inputs are finite; a program needn't handle non-finite values.
Results may differ from the reference program's by a relative error of at most 0.0031.
Values may be sent and summed in bfloat16 or wider, within the bound.
A program may use at most 128 MiB of HBM per device.

```python
import math
import jax
import jax.numpy as jnp
from jax import lax

D = 8192
FF = 28672
RANK = 512
TOKENS = 16384


def levels(stream_key, shape, pieces, smallest, top_value):
    gain, own = 1.0, jax.random.fold_in(stream_key, 6)
    for dim, shards_of in pieces:
        steps = jnp.exp(jax.random.uniform(jax.random.fold_in(own, dim), (shards_of,), jnp.float32, smallest / len(pieces), top_value / len(pieces)))
        gain = gain * jnp.repeat(steps, shape[dim] // shards_of).reshape([-1 if axis == dim else 1 for axis in range(len(shape))])
    return gain


def noise(rng, dims, spread, bound, pieces=(), held_as=jnp.bfloat16):
    result = jax.random.normal(rng, dims, jnp.float32) * spread
    if len(pieces) > 0:
        result = levels(rng, dims, pieces, -0.22, 0.18) * result
    return jnp.clip(result, min=-bound, max=bound).astype(held_as)


def setup_inputs(seed: int = 0) -> dict:
    key_of = jax.random.split(jax.random.key(seed), 6)
    return {
        "activations": noise(key_of[0], (TOKENS, D), 1.0, 6.0, ((0, 16),)),
        "out_grad": noise(key_of[1], (TOKENS, FF), (1.0 / TOKENS ** 0.5), 0.046875, ((0, 16), (1, 8))),
        "projector": noise(key_of[2], (D, RANK), D ** -0.5, 0.0625, ((0, 128),)),
        "first_moment": noise(key_of[3], (RANK, FF), 0.5, 3.0, ((0, 16), (1, 8)), jnp.float32),
        "second_moment": jnp.clip(jnp.exp(math.log(4.0) - 3.6888794 * jax.random.uniform(key_of[4], (RANK, FF), jnp.float32) ** levels(key_of[4], (RANK, FF), ((0, 16), (1, 8)), -0.2, 0.2)), 0.1, 4.0),
    }


beta_one = 0.9
beta_two = 0.999
bias_one = 1.0 - 0.9 ** 10
bias_two = 1.0 - 0.999 ** 10
adam_eps = 1e-08

def reference(activations, out_grad, projector, first_moment, second_moment):
    projected = jnp.dot(activations, projector, preferred_element_type=jnp.float32).astype(jnp.bfloat16)
    coefficients = lax.dot_general(projected, out_grad, (((0,), (0,)), ((), ())), preferred_element_type=jnp.float32)
    new_first = beta_one * first_moment + (1.0 - beta_one) * coefficients
    new_second = beta_two * second_moment + (1.0 - beta_two) * coefficients * coefficients
    normalized = (new_first / bias_one / (jnp.sqrt(new_second / bias_two) + adam_eps)).astype(jnp.bfloat16)
    update = jnp.dot(projector, normalized, preferred_element_type=jnp.float32)
    return (update, new_first, new_second)
```

```python
import jax
import jax.numpy as jnp
from jax import lax
from jax.experimental import pallas as pl
from jax.experimental.pallas import tpu as pltpu
from jax.sharding import PartitionSpec as P

beta_one = 0.9
beta_two = 0.999
bias_one = 1.0 - 0.9**10
bias_two = 1.0 - 0.999**10
adam_eps = 1e-08

MESH = pl.DeviceIdType.MESH
CHUNKS = 7
STEP = 256
NT = (((1,), (1,)), ((), ()))


def fused(act_hbm, grad_hbm, proj_ref, first_ref, second_ref,
          norm_ref, basis_ref, nfirst_ref, nsecond_ref,
          act, grad, slices, acc, pj, th_out, th_in, mine, rs_out, rs_in,
          act_sem, grad_sem, local_sem,
          a_s, a_r, b_s, b_r, f_s, f_r, c_s, c_r, t_s, t_r, r_s, r_r, g_s, g_r, h_s, h_r):
    dp = lax.axis_index("dp")
    tn = lax.axis_index("tensor")
    chip, core = dp // 2, dp % 2
    rows = proj_ref.shape[0]
    width = act.shape[2]
    cols = grad.shape[2]
    half = pj.shape[1]
    own = half // 8

    def chip_to(i):
        return ((chip // 4 + i // 4) % 2) * 4 + (chip % 4 + i % 4) % 4

    def chip_from(i):
        return ((chip // 4 + i // 4) % 2) * 4 + (chip % 4 + 4 - i % 4) % 4

    def tensor_to(i):
        return ((tn // 2 + i // 2) % 4) * 2 + (tn % 2 + i % 2) % 2

    partner = {"dp": chip * 2 + (1 - core)}

    def act_copy(k):
        return pltpu.make_async_copy(
            act_hbm.at[:, pl.ds(pl.multiple_of(k * width, 128), width)], act.at[k], act_sem.at[k])

    def grad_copy(j):
        return pltpu.make_async_copy(
            grad_hbm.at[:, pl.ds(pl.multiple_of(j * cols, 128), cols)], grad.at[j], grad_sem.at[j])

    for k in range(16):
        act_copy(k).start()
    for j in range(CHUNKS):
        grad_copy(j).start()
    my_rows = pl.ds(pl.multiple_of(tn * rows, 16), rows)
    local = pltpu.make_async_copy(proj_ref, basis_ref.at[my_rows], local_sem)
    local.start()

    barrier = pltpu.get_barrier_semaphore()
    for i in range(1, 8):
        pl.semaphore_signal(barrier, inc=1, device_id={"tensor": tensor_to(i)}, device_id_type=MESH)
        pl.semaphore_signal(barrier, inc=1, device_id={"dp": chip_to(i) * 2 + core}, device_id_type=MESH)
    pl.semaphore_signal(barrier, inc=1, device_id=partner, device_id_type=MESH)
    pl.semaphore_wait(barrier, 15)

    def a_copy(i):
        return pltpu.make_async_remote_copy(
            proj_ref, basis_ref.at[my_rows], a_s.at[i], a_r.at[i],
            device_id={"tensor": tensor_to(i)}, device_id_type=MESH)

    for i in range(1, 8):
        a_copy(i).start()
    local.wait()
    for i in range(1, 8):
        a_copy(i).wait_recv()

    ranks = slices.shape[1]
    pick = (lax.broadcasted_iota(jnp.int32, (ranks, basis_ref.shape[1]), 1)
            == lax.broadcasted_iota(jnp.int32, (ranks, basis_ref.shape[1]), 0) + tn * ranks)
    pick = jnp.where(pick, 1.0, 0.0).astype(jnp.bfloat16)
    slices[dp] = lax.dot_general(
        pick, basis_ref[...], NT, preferred_element_type=jnp.float32).astype(jnp.bfloat16)

    def b_copy(i):
        return pltpu.make_async_remote_copy(
            slices.at[dp], slices.at[dp], b_s.at[i], b_r.at[i],
            device_id={"dp": chip_to(i) * 2 + core}, device_id_type=MESH)

    b_pair = pltpu.make_async_remote_copy(
        slices.at[dp], slices.at[dp], b_s.at[0], b_r.at[0], device_id=partner, device_id_type=MESH)

    def f_copy(i):
        src = chip_from(i) * 2 + core
        return pltpu.make_async_remote_copy(
            slices.at[src], slices.at[src], f_s.at[i], f_r.at[i], device_id=partner, device_id_type=MESH)

    for i in range(1, 8):
        b_copy(i).start()
    b_pair.start()

    def wait_act(k, _):
        act_copy(k).wait()
        return 0

    lax.fori_loop(0, 16, wait_act, 0)

    def project(k):
        acc[...] += lax.dot_general(act[k], slices[k], NT, preferred_element_type=jnp.float32)

    acc[...] = jnp.zeros_like(acc)

    def near(i, _):
        @pl.when(i == 1)
        def _():
            b_pair.wait_recv()
        project(chip * 2 + (core + i) % 2)
        return 0

    lax.fori_loop(0, 2, near, 0)

    def arrived(i, _):
        b_copy(i).wait_recv()
        f_copy(i).start()
        project(chip_from(i) * 2 + core)
        return 0

    lax.fori_loop(1, 8, arrived, 0)

    def forwarded(i, _):
        f_copy(i).wait_recv()
        project(chip_from(i) * 2 + (1 - core))
        return 0

    lax.fori_loop(1, 8, forwarded, 0)

    mine_rows = pl.ds(pl.multiple_of(tn * own, 16), own)
    done = acc[...].T.astype(jnp.bfloat16)
    pj[0, mine_rows] = done[:own]
    pj[1, mine_rows] = done[own:]

    def c_copy(h, i):
        side = (core + 1 + h) % 2
        return pltpu.make_async_remote_copy(
            pj.at[side, mine_rows], pj.at[side, mine_rows], c_s.at[h, i], c_r.at[h, i],
            device_id={"tensor": tensor_to(i)}, device_id_type=MESH)

    def c_wait(h, i):
        src = ((tn // 2 + 4 - i // 2) % 4) * 2 + (tn % 2 + i % 2) % 2
        there = pl.ds(pl.multiple_of(src * own, 16), own)
        side = (core + 1) % 2 if h == 0 else core
        pltpu.make_async_remote_copy(
            pj.at[side, there], pj.at[side, there], c_s.at[h, i], c_r.at[h, i],
            device_id={"tensor": tensor_to(i)}, device_id_type=MESH).wait_recv()

    for h in range(2):
        for i in range(1, 8):
            c_copy(h, i).start()
    for j in range(CHUNKS):
        grad_copy(j).wait()

    def t_copy(j):
        return pltpu.make_async_remote_copy(
            th_out.at[j], th_in.at[j], t_s.at[j], t_r.at[j], device_id=partner, device_id_type=MESH)

    for i in range(1, 8):
        c_wait(0, i)

    def theirs(j, _):
        for s in range(0, cols, STEP):
            th_out[j, :, s:s + STEP] = jnp.dot(
                pj[1 - core], grad[j, :, s:s + STEP], preferred_element_type=jnp.float32)
        t_copy(j).start()
        return 0

    lax.fori_loop(0, CHUNKS, theirs, 0)

    for i in range(1, 8):
        c_wait(1, i)

    def r_copy(j, i):
        return pltpu.make_async_remote_copy(
            rs_out.at[j, chip_to(i)], rs_in.at[j, i], r_s.at[j, i], r_r.at[j, i],
            device_id={"dp": chip_to(i) * 2 + core}, device_id_type=MESH)

    def ours(j, _):
        t_copy(j).wait_recv()
        for s in range(0, cols, STEP):
            total = jnp.dot(pj[core], grad[j, :, s:s + STEP], preferred_element_type=jnp.float32)
            total += th_in[j, :, s:s + STEP]
            total = total.reshape(8, own, STEP)
            mine[j, :, :, s:s + STEP] = total
            rs_out[j, :, :, s:s + STEP] = total.astype(jnp.bfloat16)
        for i in range(1, 8):
            r_copy(j, i).start()
        return 0

    lax.fori_loop(0, CHUNKS, ours, 0)

    out_rows = pl.ds(pl.multiple_of(dp * own, 16), own)

    def g_copy(j, i):
        to = partner if i is None else {"dp": chip_to(i) * 2 + core}
        k = 0 if i is None else i
        return pltpu.make_async_remote_copy(
            norm_ref.at[j, out_rows], norm_ref.at[j, out_rows], g_s.at[j, k], g_r.at[j, k],
            device_id=to, device_id_type=MESH)

    def h_copy(j, i):
        there = pl.ds(pl.multiple_of((chip_from(i) * 2 + core) * own, 16), own)
        return pltpu.make_async_remote_copy(
            norm_ref.at[j, there], norm_ref.at[j, there], h_s.at[j, i], h_r.at[j, i],
            device_id=partner, device_id_type=MESH)

    def adam(j, _):
        for i in range(1, 8):
            r_copy(j, i).wait_recv()
        total = mine[j, chip]
        for i in range(1, 8):
            total += rs_in[j, i].astype(jnp.float32)
        at = pl.ds(pl.multiple_of(j * cols, 128), cols)
        new_first = beta_one * first_ref[:, at] + (1.0 - beta_one) * total
        new_second = beta_two * second_ref[:, at] + (1.0 - beta_two) * total * total
        nfirst_ref[:, at] = new_first
        nsecond_ref[:, at] = new_second
        norm_ref[j, out_rows] = (
            new_first / bias_one / (jnp.sqrt(new_second / bias_two) + adam_eps)).astype(jnp.bfloat16)
        for i in range(1, 8):
            g_copy(j, i).start()
        g_copy(j, None).start()
        return 0

    lax.fori_loop(0, CHUNKS, adam, 0)

    def pass_on(j, _):
        for i in range(1, 8):
            g_copy(j, i).wait_recv()
            h_copy(j, i).start()
        return 0

    lax.fori_loop(0, CHUNKS, pass_on, 0)

    def finish(j, _):
        g_copy(j, None).wait()
        t_copy(j).wait_send()
        for i in range(1, 8):
            h_copy(j, i).wait()
            g_copy(j, i).wait_send()
            r_copy(j, i).wait_send()
        return 0

    lax.fori_loop(0, CHUNKS, finish, 0)
    b_pair.wait_send()
    for i in range(1, 8):
        a_copy(i).wait_send()
        b_copy(i).wait_send()
        f_copy(i).wait_send()
        for h in range(2):
            c_copy(h, i).wait_send()


def decode(basis_ref, norm_ref, nf_ref, ns_ref, update_ref, nf_out, ns_out):
    update_ref[...] = jnp.dot(basis_ref[...], norm_ref[0], preferred_element_type=jnp.float32)
    nf_out[...] = nf_ref[...]
    ns_out[...] = ns_ref[...]


def per_device(activations, out_grad, projector, first_moment, second_moment):
    tokens, width = activations.shape
    ff = out_grad.shape[1]
    rows, rank = projector.shape
    own = first_moment.shape[0]
    cols = ff // CHUNKS
    half = rank // 2
    bf, f32 = jnp.bfloat16, jnp.float32
    vmem = pl.BlockSpec(memory_space=pltpu.VMEM)
    any_ = pl.BlockSpec(memory_space=pl.ANY)
    dma = pltpu.SemaphoreType.DMA
    norm, basis, nf, ns = pl.pallas_call(
        fused,
        out_shape=(
            jax.ShapeDtypeStruct((CHUNKS, rank, cols), bf),
            jax.ShapeDtypeStruct((rows * 8, rank), bf),
            jax.ShapeDtypeStruct(first_moment.shape, f32),
            jax.ShapeDtypeStruct(second_moment.shape, f32),
        ),
        in_specs=[any_, any_, vmem, vmem, vmem],
        out_specs=(vmem, vmem, vmem, vmem),
        scratch_shapes=[
            pltpu.VMEM((16, tokens, width // 16), bf),
            pltpu.VMEM((CHUNKS, tokens, cols), bf),
            pltpu.VMEM((16, rank // 8, width // 16), bf),
            pltpu.VMEM((tokens, rank // 8), f32),
            pltpu.VMEM((2, half, tokens), bf),
            pltpu.VMEM((CHUNKS, half, cols), f32),
            pltpu.VMEM((CHUNKS, half, cols), f32),
            pltpu.VMEM((CHUNKS, 8, own, cols), f32),
            pltpu.VMEM((CHUNKS, 8, own, cols), bf),
            pltpu.VMEM((CHUNKS, 8, own, cols), bf),
            dma((16,)), dma((CHUNKS,)), dma,
            dma((8,)), dma((8,)), dma((8,)), dma((8,)), dma((8,)), dma((8,)),
            dma((2, 8)), dma((2, 8)), dma((CHUNKS,)), dma((CHUNKS,)),
            dma((CHUNKS, 8)), dma((CHUNKS, 8)), dma((CHUNKS, 8)), dma((CHUNKS, 8)),
            dma((CHUNKS, 8)), dma((CHUNKS, 8)),
        ],
        compiler_params=pltpu.CompilerParams(
            collective_id=0, has_side_effects=True, vmem_limit_bytes=60 * 2**20),
        name="fused",
    )(activations, out_grad, projector, first_moment, second_moment)
    return pl.pallas_call(
        decode,
        grid=(CHUNKS,),
        out_shape=(
            jax.ShapeDtypeStruct((rows * 8, ff), f32),
            jax.ShapeDtypeStruct(first_moment.shape, f32),
            jax.ShapeDtypeStruct(second_moment.shape, f32),
        ),
        in_specs=[
            pl.BlockSpec((rows * 8, rank), lambda j: (0, 0)),
            pl.BlockSpec((1, rank, cols), lambda j: (j, 0, 0)),
            pl.BlockSpec((own, cols), lambda j: (0, j)),
            pl.BlockSpec((own, cols), lambda j: (0, j)),
        ],
        out_specs=(
            pl.BlockSpec((rows * 8, cols), lambda j: (0, j)),
            pl.BlockSpec((own, cols), lambda j: (0, j)),
            pl.BlockSpec((own, cols), lambda j: (0, j)),
        ),
        name="decode",
    )(basis, norm, nf, ns)


def solution(mesh):
    in_specs = (
        P("dp", None),
        P("dp", "tensor"),
        P(("dp", "tensor"), None),
        P("dp", "tensor"),
        P("dp", "tensor"),
    )
    out_specs = (P("dp", "tensor"), P("dp", "tensor"), P("dp", "tensor"))
    return jax.shard_map(
        per_device, mesh=mesh, in_specs=in_specs, out_specs=out_specs, check_vma=False
    )
```

```python
import jax
import jax.numpy as jnp
from jax import lax
from jax.experimental import pallas as pl
from jax.experimental.pallas import tpu as pltpu
from jax.sharding import PartitionSpec as P

beta_one = 0.9
beta_two = 0.999
bias_one = 1.0 - 0.9**10
bias_two = 1.0 - 0.999**10
adam_eps = 1e-08

MESH = pl.DeviceIdType.MESH
CHUNKS = 4
UNITS = 2 * CHUNKS
STEP = 256
LAGS = (2, 2, 0, 2, 4)
SLOTS = 3
NT = (((1,), (1,)), ((), ()))


def fused(act_hbm, grad_hbm, proj_hbm, first_hbm, second_hbm,
          norm, basis, nfirst, nsecond,
          act, grad, proj, part, first, second, slices, acc, pj, res, th_in, out1, in1, out2, in2,
          act_sem, grad_sem, local_sem, sent_sem, once_sem,
          b_r, f_r, c_r, t_r, p_r, q_r, g_r, h_r):
    dp = lax.axis_index("dp")
    tn = lax.axis_index("tensor")
    chip, core = dp // 2, dp % 2
    yh, zz = chip // 4, chip % 4
    rows = proj.shape[0]
    width = act.shape[2]
    cols = grad.shape[2]
    own = first.shape[0] // 2

    def chip_to(i):
        return ((yh + i // 4) % 2) * 4 + (zz + i % 4) % 4

    def chip_from(i):
        return ((yh + i // 4) % 2) * 4 + (zz + 4 - i % 4) % 4

    def tensor_to(i):
        return ((tn // 2 + i // 2) % 4) * 2 + (tn % 2 + i % 2) % 2

    def tensor_from(i):
        return ((tn // 2 + 4 - i // 2) % 4) * 2 + (tn % 2 + i % 2) % 2

    def at_chip(i):
        return {"dp": chip_to(i) * 2 + core}

    partner = {"dp": chip * 2 + (1 - core)}

    def remote(src, dst, send, recv, to):
        return pltpu.make_async_remote_copy(src, dst, send, recv, device_id=to, device_id_type=MESH)

    def arrive(ref, sem):
        pltpu.make_async_copy(ref, ref, sem).wait()

    a_s, b_s, f_s, c_s, e_s, t_s, p_s, d_s = (sent_sem.at[i] for i in range(8))
    a_r, e_r, n_s, n_r, d_r = (once_sem.at[i] for i in range(5))

    def act_copy(k):
        return pltpu.make_async_copy(
            act_hbm.at[:, pl.ds(pl.multiple_of(k * width, 128), width)], act.at[k], act_sem.at[k])

    def grad_copy(j):
        return pltpu.make_async_copy(
            grad_hbm.at[:, pl.ds(pl.multiple_of(j * cols, 128), cols)], grad.at[j], grad_sem)

    barrier = pltpu.get_barrier_semaphore()
    for i in range(1, 8):
        pl.semaphore_signal(barrier, inc=1, device_id={"tensor": tensor_to(i)}, device_id_type=MESH)
        pl.semaphore_signal(barrier, inc=1, device_id=at_chip(i), device_id_type=MESH)
    pl.semaphore_signal(barrier, inc=1, device_id=partner, device_id_type=MESH)

    proj_copy = pltpu.make_async_copy(proj_hbm, proj, local_sem.at[0])
    first_copy = pltpu.make_async_copy(first_hbm, first, local_sem.at[1])
    second_copy = pltpu.make_async_copy(second_hbm, second, local_sem.at[2])
    proj_copy.start()
    my_rows = pl.ds(pl.multiple_of(tn * rows, 16), rows)
    proj_copy.wait()
    for c in (core, 1 - core):
        act_copy(chip * 2 + c).start()
    for i in range(1, 8):
        for c in (core, 1 - core):
            act_copy(chip_from(i) * 2 + c).start()
    for j in range(CHUNKS):
        grad_copy(j).start()
    first_copy.start()
    second_copy.start()

    with jax.named_scope("barrier_wait"):
        pl.semaphore_wait(barrier, 15)

    def lanes(t):
        return pl.ds(pl.multiple_of((t // 2) * 128, 128), 128)

    def a_copy(i):
        return remote(proj.at[:, lanes(tensor_to(i))], part.at[my_rows], a_s, a_r,
                      {"tensor": tensor_to(i)})

    e_near = remote(proj, basis.at[my_rows], n_s, n_r, {"tensor": tensor_to(1)})

    def e_copy(i, x):
        there = pl.ds(pl.multiple_of(x * 2 * rows, 16), 2 * rows)
        return remote(basis.at[there], basis.at[there], e_s, e_r, {"tensor": tensor_to(2 * i)})

    for i in range(1, 8):
        a_copy(i).start()
    e_near.start()
    part[my_rows] = proj[:, lanes(tn)]
    basis[my_rows] = proj[...]
    ranks = slices.shape[1]
    pick = (lax.broadcasted_iota(jnp.int32, (ranks, 128), 1)
            == lax.broadcasted_iota(jnp.int32, (ranks, 128), 0) + (tn % 2) * ranks)
    pick = jnp.where(pick, 1.0, 0.0).astype(jnp.bfloat16)
    with jax.named_scope("a_wait"):
        arrive(part.at[0:7 * rows], a_r)

    slices[dp] = lax.dot_general(
        pick, part[...], NT, preferred_element_type=jnp.float32).astype(jnp.bfloat16)

    def b_copy(i):
        return remote(slices.at[dp], slices.at[dp], b_s, b_r.at[i], at_chip(i))

    b_pair = remote(slices.at[dp], slices.at[dp], b_s, b_r.at[0], partner)

    def f_copy(i):
        src = chip_from(i) * 2 + core
        return remote(slices.at[src], slices.at[src], f_s, f_r.at[i], partner)

    for i in range(1, 8):
        b_copy(i).start()
    b_pair.start()

    def product(k):
        act_copy(k).wait()
        return lax.dot_general(act[k], slices[k], NT, preferred_element_type=jnp.float32)

    def project(k):
        acc[...] += product(k)

    with jax.named_scope("near"):
        acc[...] = product(dp)
        b_pair.wait_recv()
        project(chip * 2 + (1 - core))

    def arrived(i, _):
        @pl.when(i < 8)
        def _():
            b_copy(i).wait_recv()
            f_copy(i).start()
            project(chip_from(i) * 2 + core)

        @pl.when(i > 1)
        def _():
            f_copy(i - 1).wait_recv()
            project(chip_from(i - 1) * 2 + (1 - core))
        return 0

    with jax.named_scope("arrived"):
        lax.fori_loop(1, 9, arrived, 0)

    def block(t):
        return pl.ds(pl.multiple_of(t * own, 16), own)

    done = acc[...].T.astype(jnp.bfloat16)
    for c in range(2):
        for u in range(2):
            pj[u, c, block(tn)] = done[(2 * c + u) * own:(2 * c + u + 1) * own]

    def c_copy(u, i, t):
        return remote(pj.at[u, :, block(t)], pj.at[u, :, block(t)], c_s, c_r.at[u],
                      {"tensor": tensor_to(i)})

    def c_wait(u):
        arrive(pj.at[u, :, 0:7 * own], c_r.at[u])

    for u in range(2):
        for i in range(1, 8):
            c_copy(u, i, tn).start()
    arrive(grad, grad_sem)
    e_near.wait_recv()
    for i in range(1, 4):
        e_copy(i, tn // 2).start()

    def t_copy(n):
        return remote(res.at[n, 1 - core], th_in.at[n], t_s, t_r.at[n], partner)

    def dots(n):
        left = pj[n // CHUNKS].reshape(16 * own, acc.shape[0])
        for s in range(0, cols, STEP):
            w = min(STEP, cols - s)
            res[n, :, :, :, :, s:s + w] = jnp.dot(
                left, grad[n % CHUNKS, :, s:s + w], preferred_element_type=jnp.float32
            ).reshape(2, 2, 4, own, w)
        t_copy(n).start()

    def p_y(j):
        return remote(out1.at[j, 1 - yh], in1.at[j, :, 0], p_s, p_r.at[j], at_chip(4))

    def p_z(j, i):
        return remote(out1.at[j, :, (zz + i) % 4], in1.at[j, i], p_s, p_r.at[j], at_chip(i))

    def q_z(j, i):
        return remote(out2.at[j, (zz + i) % 4], in2.at[j, i], p_s, q_r.at[j], at_chip(i))

    def q_y(j):
        return remote(out2.at[j, 1 - yh], in2.at[j, 0], p_s, q_r.at[j], at_chip(4))

    def g_z(j, i, z):
        return remote(norm.at[j, core, yh, z], norm.at[j, core, yh, z], p_s, g_r.at[j], at_chip(i))

    def g_y(j, y):
        return remote(norm.at[j, core, y, zz], norm.at[j, core, y, zz], p_s, g_r.at[j], at_chip(4))

    def h_y(j, y):
        return remote(norm.at[j, core, y], norm.at[j, core, y], p_s, h_r.at[j], at_chip(4))

    def h_z(j, i, z):
        return remote(norm.at[j, core, :, z], norm.at[j, core, :, z], p_s, h_r.at[j], at_chip(i))

    def d_copy(j, c):
        return remote(norm.at[j, c], norm.at[j, c], d_s, d_r, partner)

    def y_first(n):
        return pl.when(n % 2 == 1)

    def z_first(n):
        return pl.when(n % 2 == 0)

    def combine(n):
        t_copy(n).wait_recv()

        @y_first(n)
        def _():
            out1[n, 1 - yh] = (res[n, core, 1 - yh] + th_in[n, 1 - yh]).astype(jnp.bfloat16)
            p_y(n).start()

        @z_first(n)
        def _():
            for i in range(1, 4):
                z = (zz + i) % 4
                out1[n, :, z] = (res[n, core, :, z] + th_in[n, :, z]).astype(jnp.bfloat16)
                p_z(n, i).start()

    def stage_one(j):
        @y_first(j)
        def _():
            p_y(j).wait_recv()
            total = res[j, core, yh] + th_in[j, yh] + in1[j, :, 0].astype(jnp.float32)
            res[j, core, yh] = total
            out2[j] = total.astype(jnp.bfloat16)
            for i in range(1, 4):
                q_z(j, i).start()

        @z_first(j)
        def _():
            total = res[j, core, :, zz] + th_in[j, :, zz]
            arrive(in1.at[j, 1:4], p_r.at[j])
            for i in range(1, 4):
                total += in1[j, i].astype(jnp.float32)
            res[j, core, :, zz] = total
            out2[j, 0:2] = total.astype(jnp.bfloat16)
            q_y(j).start()

    def adam(j):
        @y_first(j)
        def _():
            total = res[j, core, yh, zz]
            arrive(in2.at[j, 1:4], q_r.at[j])
            for i in range(1, 4):
                total += in2[j, i].astype(jnp.float32)
            res[j, core, yh, zz] = total

        @z_first(j)
        def _():
            q_y(j).wait_recv()
            res[j, core, yh, zz] = res[j, core, yh, zz] + in2[j, 0].astype(jnp.float32)

        total = res[j, core, yh, zz]
        at = (pl.ds(pl.multiple_of((j // CHUNKS) * own, 8), own),
              pl.ds(pl.multiple_of((j % CHUNKS) * cols, 128), cols))
        new_first = beta_one * first[at] + (1.0 - beta_one) * total
        new_second = beta_two * second[at] + (1.0 - beta_two) * total * total
        nfirst[at] = new_first
        nsecond[at] = new_second
        norm[j, core, yh, zz] = (
            new_first / bias_one / (jnp.sqrt(new_second / bias_two) + adam_eps)).astype(jnp.bfloat16)

        @y_first(j)
        def _():
            for i in range(1, 4):
                g_z(j, i, zz).start()

        @z_first(j)
        def _():
            g_y(j, yh).start()

    def stage_two(j):
        @y_first(j)
        def _():
            arrive(norm.at[j, core, yh, 0:3], g_r.at[j])
            h_y(j, yh).start()

        @z_first(j)
        def _():
            g_y(j, 1 - yh).wait_recv()
            for i in range(1, 4):
                h_z(j, i, zz).start()

    def to_pair(j):
        @y_first(j)
        def _():
            h_y(j, 1 - yh).wait_recv()

        @z_first(j)
        def _():
            arrive(norm.at[j, core, :, 0:3], h_r.at[j])

        d_copy(j, core).start()

    def loop(steps, *stages):
        def body(k, _):
            for name, do, lag, first_unit, count in stages:
                @pl.when(jnp.logical_and(k >= lag, k < lag + count))
                def _():
                    with jax.named_scope(name):
                        do(first_unit + k - lag)
            return 0

        lax.fori_loop(0, steps, body, 0)

    with jax.named_scope("c_wait0"):
        c_wait(0)
    loop(CHUNKS + LAGS[0], ("dots", dots, 0, 0, CHUNKS), ("combine", combine, LAGS[0], 0, CHUNKS))
    with jax.named_scope("c_wait1"):
        c_wait(1)
    loop(CHUNKS + max(LAGS[:2]), ("dots", dots, 0, CHUNKS, CHUNKS), ("combine", combine, LAGS[0], CHUNKS, CHUNKS),
         ("one", stage_one, LAGS[1], 0, CHUNKS))
    first_copy.wait()
    second_copy.wait()
    loop(UNITS + LAGS[4], ("one", stage_one, 0, CHUNKS, CHUNKS), ("adam", adam, LAGS[2], 0, UNITS),
         ("two", stage_two, LAGS[3], 0, UNITS), ("pair", to_pair, LAGS[4], 0, UNITS))

    with jax.named_scope("finish"):
        arrive(part.at[0:7 * rows], a_s)
        arrive(slices.at[0:8], b_s)
        arrive(slices.at[0:7], f_s)
        arrive(pj.at[:, :, 0:7 * own], c_s)
        e_near.wait_send()
        arrive(basis.at[0:6 * rows], e_s)
        arrive(basis.at[0:6 * rows], e_r)
        arrive(res.at[:, 0], t_s)
        arrive(norm.at[0:UNITS * 14 // 16], p_s)
        arrive(norm.at[:, 0], d_s)
        arrive(norm.at[:, 0], d_r)


def decode(basis, norm, nf, ns, update, nf_out, ns_out, buf, sem, small_sem):
    cols = norm.shape[5]
    nf_copy = pltpu.make_async_copy(nf, nf_out, small_sem.at[0])
    ns_copy = pltpu.make_async_copy(ns, ns_out, small_sem.at[1])

    def out_copy(j):
        return pltpu.make_async_copy(
            buf.at[j % SLOTS], update.at[:, pl.ds(pl.multiple_of(j * cols, 128), cols)], sem.at[j % SLOTS])

    def step(j, _):
        @pl.when(j >= SLOTS)
        def _():
            out_copy(j - SLOTS).wait()
        block = jnp.concatenate(
            [norm[u * CHUNKS + j, c, y, z]
             for y in range(2) for z in range(4) for c in range(2) for u in range(2)], axis=0)
        buf[j % SLOTS] = jnp.dot(basis[...], block, preferred_element_type=jnp.float32)
        out_copy(j).start()
        return 0

    lax.fori_loop(0, CHUNKS, step, 0)
    nf_copy.start()
    ns_copy.start()
    for j in range(CHUNKS - SLOTS, CHUNKS):
        out_copy(j).wait()
    nf_copy.wait()
    ns_copy.wait()


def per_device(activations, out_grad, projector, first_moment, second_moment):
    tokens, width = activations.shape
    ff = out_grad.shape[1]
    rows, rank = projector.shape
    own = first_moment.shape[0] // 2
    cols = ff // CHUNKS
    half = rank // 2
    bf, f32 = jnp.bfloat16, jnp.float32
    vmem = pl.BlockSpec(memory_space=pltpu.VMEM)
    any_ = pl.BlockSpec(memory_space=pl.ANY)
    dma = pltpu.SemaphoreType.DMA
    norm, basis, nf, ns = pl.pallas_call(
        fused,
        out_shape=(
            pltpu.VMEM((UNITS, 2, 2, 4, own, cols), bf),
            pltpu.VMEM((rows * 8, rank), bf),
            pltpu.VMEM(first_moment.shape, f32),
            pltpu.VMEM(second_moment.shape, f32),
        ),
        in_specs=[any_] * 5,
        out_specs=(vmem, vmem, vmem, vmem),
        scratch_shapes=[
            pltpu.VMEM((16, tokens, width // 16), bf),
            pltpu.VMEM((CHUNKS, tokens, cols), bf),
            pltpu.VMEM((rows, rank), bf),
            pltpu.VMEM((rows * 8, 128), bf),
            pltpu.VMEM(first_moment.shape, f32),
            pltpu.VMEM(second_moment.shape, f32),
            pltpu.VMEM((16, rank // 8, width // 16), bf),
            pltpu.VMEM((tokens, rank // 8), f32),
            pltpu.VMEM((2, 2, half // 2, tokens), bf),
            pltpu.VMEM((UNITS, 2, 2, 4, own, cols), f32),
            pltpu.VMEM((UNITS, 2, 4, own, cols), f32),
            pltpu.VMEM((UNITS, 2, 4, own, cols), bf),
            pltpu.VMEM((UNITS, 4, 2, own, cols), bf),
            pltpu.VMEM((UNITS, 4, own, cols), bf),
            pltpu.VMEM((UNITS, 4, own, cols), bf),
            dma((16,)), dma, dma((3,)), dma((8,)), dma((5,)),
            dma((8,)), dma((8,)), dma((2,)), dma((UNITS,)),
            dma((UNITS,)), dma((UNITS,)), dma((UNITS,)), dma((UNITS,)),
        ],
        compiler_params=pltpu.CompilerParams(
            collective_id=0, has_side_effects=True, vmem_limit_bytes=54 * 2**20),
        name="fused",
    )(activations, out_grad, projector, first_moment, second_moment)
    return pl.pallas_call(
        decode,
        out_shape=(
            jax.ShapeDtypeStruct((rows * 8, ff), f32),
            jax.ShapeDtypeStruct(first_moment.shape, f32),
            jax.ShapeDtypeStruct(second_moment.shape, f32),
        ),
        in_specs=[vmem] * 4,
        out_specs=(any_, any_, any_),
        scratch_shapes=[
            pltpu.VMEM((SLOTS, rows * 8, cols), f32),
            dma((SLOTS,)), dma((2,)),
        ],
        compiler_params=pltpu.CompilerParams(vmem_limit_bytes=16 * 2**20),
        name="decode",
    )(basis, norm, nf, ns)


def solution(mesh):
    in_specs = (
        P("dp", None),
        P("dp", "tensor"),
        P(("dp", "tensor"), None),
        P("dp", "tensor"),
        P("dp", "tensor"),
    )
    out_specs = (P("dp", "tensor"), P("dp", "tensor"), P("dp", "tensor"))
    return jax.shard_map(
        per_device, mesh=mesh, in_specs=in_specs, out_specs=out_specs, check_vma=False
    )
```

```python
import jax
import jax.numpy as jnp
from jax import lax
from jax.experimental import pallas as pl
from jax.experimental.pallas import tpu as pltpu
from jax.sharding import PartitionSpec as P

beta_one = 0.9
beta_two = 0.999
bias_one = 1.0 - 0.9**10
bias_two = 1.0 - 0.999**10
adam_eps = 1e-08

MESH = pl.DeviceIdType.MESH
CHUNKS = 7
CHIP_ORDER = (1, 3, 4, 5, 7, 2, 6)
TENSOR_ORDER = (5, 3, 7, 4, 2, 6, 1)
Z_ORDER = (1, 2, 3)
UNITS = 2 * CHUNKS
STEP = 256
LAGS = (2, 3, 0, 6, 11)
SLOTS = 3
NT = (((1,), (1,)), ((), ()))


def fused(act_hbm, grad_hbm, proj_hbm, first_hbm, second_hbm,
          norm, basis, nfirst, nsecond,
          act, grad, proj, part, first, second, slices, acc, pj, res, th_in, out1, in1, out2, in2, total_sent,
          act_sem, grad_sem, local_sem, sent_sem, once_sem,
          b_r, f_r, c_r, t_r, p_r, q_r, g_r, h_r):
    dp = lax.axis_index("dp")
    tn = lax.axis_index("tensor")
    chip, core = dp // 2, dp % 2
    yh, zz = chip // 4, chip % 4
    rows = proj.shape[0]
    width = act.shape[2]
    cols = grad.shape[2]
    own = first.shape[0] // 2

    def chip_to(i):
        return ((yh + i // 4) % 2) * 4 + (zz + i % 4) % 4

    def chip_from(i):
        return ((yh + i // 4) % 2) * 4 + (zz + 4 - i % 4) % 4

    def tensor_to(i):
        return ((tn // 2 + i // 2) % 4) * 2 + (tn % 2 + i % 2) % 2

    def tensor_from(i):
        return ((tn // 2 + 4 - i // 2) % 4) * 2 + (tn % 2 + i % 2) % 2

    def at_chip(i):
        return {"dp": chip_to(i) * 2 + core}

    partner = {"dp": chip * 2 + (1 - core)}

    def remote(src, dst, send, recv, to):
        return pltpu.make_async_remote_copy(src, dst, send, recv, device_id=to, device_id_type=MESH)

    def arrive(ref, sem):
        pltpu.make_async_copy(ref, ref, sem).wait()

    a_s, b_s, f_s, c_s, e_s, t_s, p_s, d_s = (sent_sem.at[i] for i in range(8))
    a_r, e_r, n_s, n_r, d_r = (once_sem.at[i] for i in range(5))

    def act_copy(k):
        return pltpu.make_async_copy(
            act_hbm.at[:, pl.ds(pl.multiple_of(k * width, 128), width)], act.at[k], act_sem.at[k])

    def grad_copy(j):
        return pltpu.make_async_copy(
            grad_hbm.at[:, pl.ds(pl.multiple_of(j * cols, 128), cols)], grad.at[j], grad_sem)

    barrier = pltpu.get_barrier_semaphore()
    for i, k in zip(CHIP_ORDER, TENSOR_ORDER):
        pl.semaphore_signal(barrier, inc=1, device_id=at_chip(i), device_id_type=MESH)
        pl.semaphore_signal(barrier, inc=1, device_id={"tensor": tensor_to(k)}, device_id_type=MESH)
    pl.semaphore_signal(barrier, inc=1, device_id=partner, device_id_type=MESH)

    proj_copy = pltpu.make_async_copy(proj_hbm, proj, local_sem.at[0])
    first_copy = pltpu.make_async_copy(first_hbm, first, local_sem.at[1])
    second_copy = pltpu.make_async_copy(second_hbm, second, local_sem.at[2])
    proj_copy.start()
    my_rows = pl.ds(pl.multiple_of(tn * rows, 16), rows)
    proj_copy.wait()
    for c in (core, 1 - core):
        act_copy(chip * 2 + c).start()
    for i in CHIP_ORDER:
        for c in (core, 1 - core):
            act_copy(chip_from(i) * 2 + c).start()
    for j in range(CHUNKS):
        grad_copy(j).start()
    first_copy.start()
    second_copy.start()

    with jax.named_scope("barrier_wait"):
        pl.semaphore_wait(barrier, 15)

    def lanes(t):
        return pl.ds(pl.multiple_of((t // 2) * 128, 128), 128)

    def a_copy(i):
        return remote(proj.at[:, lanes(tensor_to(i))], part.at[my_rows], a_s, a_r,
                      {"tensor": tensor_to(i)})

    e_near = remote(proj, basis.at[my_rows], n_s, n_r, {"tensor": tensor_to(1)})

    def e_copy(i, x):
        there = pl.ds(pl.multiple_of(x * 2 * rows, 16), 2 * rows)
        return remote(basis.at[there], basis.at[there], e_s, e_r, {"tensor": tensor_to(2 * i)})

    for i in TENSOR_ORDER:
        a_copy(i).start()
    e_near.start()
    part[my_rows] = proj[:, lanes(tn)]
    basis[my_rows] = proj[...]
    ranks = slices.shape[1]
    pick = (lax.broadcasted_iota(jnp.int32, (ranks, 128), 1)
            == lax.broadcasted_iota(jnp.int32, (ranks, 128), 0) + (tn % 2) * ranks)
    pick = jnp.where(pick, 1.0, 0.0).astype(jnp.bfloat16)
    with jax.named_scope("a_wait"):
        arrive(part.at[0:7 * rows], a_r)

    slices[dp] = lax.dot_general(
        pick, part[...], NT, preferred_element_type=jnp.float32).astype(jnp.bfloat16)

    def b_copy(i):
        return remote(slices.at[dp], slices.at[dp], b_s, b_r.at[i], at_chip(i))

    b_pair = remote(slices.at[dp], slices.at[dp], b_s, b_r.at[0], partner)

    def f_copy(i):
        src = chip_from(i) * 2 + core
        return remote(slices.at[src], slices.at[src], f_s, f_r.at[i], partner)

    for i in CHIP_ORDER:
        b_copy(i).start()
    b_pair.start()

    def product(k):
        act_copy(k).wait()
        return lax.dot_general(slices[k], act[k], NT, preferred_element_type=jnp.float32)

    def project(k):
        acc[...] += product(k)

    with jax.named_scope("near"):
        acc[...] = product(dp)
        b_pair.wait_recv()
        project(chip * 2 + (1 - core))

    with jax.named_scope("arrived"):
        for i, before in zip(CHIP_ORDER + (None,), (None,) + CHIP_ORDER):
            if i is not None:
                b_copy(i).wait_recv()
                f_copy(i).start()
                project(chip_from(i) * 2 + core)
            if before is not None:
                f_copy(before).wait_recv()
                project(chip_from(before) * 2 + (1 - core))

    def block(t):
        return pl.ds(pl.multiple_of(t * own, 16), own)

    done = acc[...].astype(jnp.bfloat16)
    for c in range(2):
        for u in range(2):
            pj[u, c, block(tn)] = done[(2 * c + u) * own:(2 * c + u + 1) * own]

    def c_copy(i):
        return remote(pj.at[1, :, block(tn)], pj.at[1, :, block(tn)], c_s, c_r.at[2],
                      {"tensor": tensor_to(i)})

    def c_half(side, i, k):
        return remote(pj.at[0, side, block(tn)], pj.at[0, side, block(tn)], c_s, c_r.at[k],
                      {"tensor": tensor_to(i)})

    for k, side in ((0, 1 - core), (1, core)):
        for i in range(1, 8):
            c_half(side, i, k).start()
    for i in range(1, 8):
        c_copy(i).start()
    arrive(grad, grad_sem)
    e_near.wait_recv()
    for i in Z_ORDER:
        e_copy(i, tn // 2).start()

    def t_copy(n):
        return remote(res.at[n, 1 - core], th_in.at[n], t_s, t_r.at[n], partner)

    def half_dots(n, side):
        for s in range(0, cols, STEP):
            w = min(STEP, cols - s)
            res[n, side, :, :, :, s:s + w] = jnp.dot(
                pj[0, side], grad[n, :, s:s + w], preferred_element_type=jnp.float32
            ).reshape(2, 4, own, w)

    def theirs(n):
        half_dots(n, 1 - core)
        t_copy(n).start()

    def mine(n):
        half_dots(n, core)

    def dots(n):
        left = pj[1].reshape(16 * own, acc.shape[1])
        for s in range(0, cols, STEP):
            w = min(STEP, cols - s)
            res[n, :, :, :, :, s:s + w] = jnp.dot(
                left, grad[n - CHUNKS, :, s:s + w], preferred_element_type=jnp.float32
            ).reshape(2, 2, 4, own, w)
        t_copy(n).start()

    def p_y(j):
        return remote(out1.at[j, 1 - yh], in1.at[j, :, 0], p_s, p_r.at[j], at_chip(4))

    def p_z(j, i):
        return remote(out1.at[j, :, (zz + i) % 4], in1.at[j, i], p_s, p_r.at[j], at_chip(i))

    def q_z(j, i):
        return remote(out2.at[j, (zz + i) % 4], in2.at[j, i], p_s, q_r.at[j], at_chip(i))

    def q_y(j):
        return remote(out2.at[j, 1 - yh], in2.at[j, 0], p_s, q_r.at[j], at_chip(4))

    def g_z(j, i, z):
        return remote(norm.at[j, core, yh, z], norm.at[j, core, yh, z], p_s, g_r.at[j], at_chip(i))

    def g_y(j, y):
        return remote(norm.at[j, core, y, zz], norm.at[j, core, y, zz], p_s, g_r.at[j], at_chip(4))

    def h_y(j, y):
        return remote(norm.at[j, core, y], norm.at[j, core, y], p_s, h_r.at[j], at_chip(4))

    def h_z(j, i, z):
        return remote(norm.at[j, core, :, z], norm.at[j, core, :, z], p_s, h_r.at[j], at_chip(i))

    def d_copy(j, c):
        return remote(norm.at[j, c], norm.at[j, c], d_s, d_r, partner)

    def reduce_z(n):
        return n % 2 == 0

    def gather_y(n):
        return n % 2 == 1

    def y_first(n):
        return pl.when(jnp.logical_not(reduce_z(n)))

    def z_first(n):
        return pl.when(reduce_z(n))

    def then_y(n):
        return pl.when(jnp.logical_not(gather_y(n)))

    def then_z(n):
        return pl.when(gather_y(n))

    def combine(n):
        t_copy(n).wait_recv()

        @y_first(n)
        def _():
            out1[n, 1 - yh] = (res[n, core, 1 - yh] + th_in[n, 1 - yh]).astype(jnp.bfloat16)
            p_y(n).start()

        @z_first(n)
        def _():
            for i in Z_ORDER:
                z = (zz + i) % 4
                out1[n, :, z] = (res[n, core, :, z] + th_in[n, :, z]).astype(jnp.bfloat16)
                p_z(n, i).start()

    def stage_one(j):
        @y_first(j)
        def _():
            p_y(j).wait_recv()
            total = res[j, core, yh] + th_in[j, yh] + in1[j, :, 0].astype(jnp.float32)
            res[j, core, yh] = total
            out2[j] = total.astype(jnp.bfloat16)
            for i in Z_ORDER:
                q_z(j, i).start()

        @z_first(j)
        def _():
            total = res[j, core, :, zz] + th_in[j, :, zz]
            arrive(in1.at[j, 1:4], p_r.at[j])
            for i in range(1, 4):
                total += in1[j, i].astype(jnp.float32)
            res[j, core, :, zz] = total
            out2[j, 0:2] = total.astype(jnp.bfloat16)
            q_y(j).start()

    def adam(j):
        @y_first(j)
        def _():
            total = res[j, core, yh, zz]
            arrive(in2.at[j, 1:4], q_r.at[j])
            for i in range(1, 4):
                total += in2[j, i].astype(jnp.float32)
            res[j, core, yh, zz] = total

        @z_first(j)
        def _():
            q_y(j).wait_recv()
            res[j, core, yh, zz] = res[j, core, yh, zz] + in2[j, 0].astype(jnp.float32)

        total = res[j, core, yh, zz]
        at = (pl.ds(pl.multiple_of((j // CHUNKS) * own, 8), own),
              pl.ds(pl.multiple_of((j % CHUNKS) * cols, 128), cols))
        new_first = beta_one * first[at] + (1.0 - beta_one) * total
        new_second = beta_two * second[at] + (1.0 - beta_two) * total * total
        nfirst[at] = new_first
        nsecond[at] = new_second
        norm[j, core, yh, zz] = (
            new_first / bias_one / (jnp.sqrt(new_second / bias_two) + adam_eps)).astype(jnp.bfloat16)

        @then_y(j)
        def _():
            for i in Z_ORDER:
                g_z(j, i, zz).start()

        @then_z(j)
        def _():
            g_y(j, yh).start()

    def stage_two(j):
        @then_y(j)
        def _():
            arrive(norm.at[j, core, yh, 0:3], g_r.at[j])
            h_y(j, yh).start()

        @then_z(j)
        def _():
            g_y(j, 1 - yh).wait_recv()
            for i in Z_ORDER:
                h_z(j, i, zz).start()

    def to_pair(j):
        @then_y(j)
        def _():
            h_y(j, 1 - yh).wait_recv()

        @then_z(j)
        def _():
            arrive(norm.at[j, core, :, 0:3], h_r.at[j])

        d_copy(j, core).start()

    def loop(steps, *stages):
        def body(k, _):
            for name, do, lag, first_unit, count in stages:
                @pl.when(jnp.logical_and(k >= lag, k < lag + count))
                def _():
                    with jax.named_scope(name):
                        do(first_unit + k - lag)
            return 0

        lax.fori_loop(0, steps, body, 0)

    with jax.named_scope("c_wait0"):
        arrive(pj.at[0, 0, 0:7 * own], c_r.at[0])
    loop(CHUNKS, ("theirs", theirs, 0, 0, CHUNKS))
    with jax.named_scope("c_wait1"):
        arrive(pj.at[0, 0, 0:7 * own], c_r.at[1])
    loop(CHUNKS, ("dots", mine, 0, 0, CHUNKS), ("combine", combine, 0, 0, CHUNKS))
    with jax.named_scope("c_wait1"):
        arrive(pj.at[1, :, 0:7 * own], c_r.at[2])
    loop(CHUNKS + max(LAGS[:2]), ("dots", dots, 0, CHUNKS, CHUNKS), ("combine", combine, LAGS[0], CHUNKS, CHUNKS),
         ("one", stage_one, LAGS[1], 0, CHUNKS))
    first_copy.wait()
    second_copy.wait()
    loop(UNITS + LAGS[4], ("one", stage_one, 0, CHUNKS, CHUNKS), ("adam", adam, LAGS[2], 0, UNITS),
         ("two", stage_two, LAGS[3], 0, UNITS), ("pair", to_pair, LAGS[4], 0, UNITS))

    with jax.named_scope("finish"):
        arrive(part.at[0:7 * rows], a_s)
        arrive(slices.at[0:8], b_s)
        arrive(slices.at[0:7], f_s)
        arrive(pj.at[:, :, 0:7 * own], c_s)
        e_near.wait_send()
        arrive(basis.at[0:6 * rows], e_s)
        arrive(basis.at[0:6 * rows], e_r)
        arrive(res.at[:, 0], t_s)
        arrive(total_sent, p_s)
        arrive(norm.at[:, 0], d_s)
        arrive(norm.at[:, 0], d_r)


def decode(basis, norm, nf, ns, update, nf_out, ns_out, buf, sem, small_sem):
    cols = norm.shape[5]
    nf_copy = pltpu.make_async_copy(nf, nf_out, small_sem.at[0])
    ns_copy = pltpu.make_async_copy(ns, ns_out, small_sem.at[1])

    def out_copy(j):
        return pltpu.make_async_copy(
            buf.at[j % SLOTS], update.at[:, pl.ds(pl.multiple_of(j * cols, 128), cols)], sem.at[j % SLOTS])

    def step(j, _):
        @pl.when(j >= SLOTS)
        def _():
            out_copy(j - SLOTS).wait()
        block = jnp.concatenate(
            [norm[u * CHUNKS + j, c, y, z]
             for y in range(2) for z in range(4) for c in range(2) for u in range(2)], axis=0)
        buf[j % SLOTS] = jnp.dot(basis[...], block, preferred_element_type=jnp.float32)
        out_copy(j).start()
        return 0

    lax.fori_loop(0, CHUNKS, step, 0)
    nf_copy.start()
    ns_copy.start()
    for j in range(CHUNKS - SLOTS, CHUNKS):
        out_copy(j).wait()
    nf_copy.wait()
    ns_copy.wait()


def per_device(activations, out_grad, projector, first_moment, second_moment):
    tokens, width = activations.shape
    ff = out_grad.shape[1]
    rows, rank = projector.shape
    own = first_moment.shape[0] // 2
    cols = ff // CHUNKS
    half = rank // 2
    bf, f32 = jnp.bfloat16, jnp.float32
    vmem = pl.BlockSpec(memory_space=pltpu.VMEM)
    any_ = pl.BlockSpec(memory_space=pl.ANY)
    dma = pltpu.SemaphoreType.DMA
    norm, basis, nf, ns = pl.pallas_call(
        fused,
        out_shape=(
            pltpu.VMEM((UNITS, 2, 2, 4, own, cols), bf),
            pltpu.VMEM((rows * 8, rank), bf),
            pltpu.VMEM(first_moment.shape, f32),
            pltpu.VMEM(second_moment.shape, f32),
        ),
        in_specs=[any_] * 5,
        out_specs=(vmem, vmem, vmem, vmem),
        scratch_shapes=[
            pltpu.VMEM((16, tokens, width // 16), bf),
            pltpu.VMEM((CHUNKS, tokens, cols), bf),
            pltpu.VMEM((rows, rank), bf),
            pltpu.VMEM((rows * 8, 128), bf),
            pltpu.VMEM(first_moment.shape, f32),
            pltpu.VMEM(second_moment.shape, f32),
            pltpu.VMEM((16, rank // 8, width // 16), bf),
            pltpu.VMEM((rank // 8, tokens), f32),
            pltpu.VMEM((2, 2, half // 2, tokens), bf),
            pltpu.VMEM((UNITS, 2, 2, 4, own, cols), f32),
            pltpu.VMEM((UNITS, 2, 4, own, cols), f32),
            pltpu.VMEM((UNITS, 2, 4, own, cols), bf),
            pltpu.VMEM((UNITS, 4, 2, own, cols), bf),
            pltpu.VMEM((UNITS, 4, own, cols), bf),
            pltpu.VMEM((UNITS, 4, own, cols), bf),
            pltpu.VMEM((UNITS, 14, own, cols), bf),
            dma((16,)), dma, dma((3,)), dma((8,)), dma((5,)),
            dma((8,)), dma((8,)), dma((3,)), dma((UNITS,)),
            dma((UNITS,)), dma((UNITS,)), dma((UNITS,)), dma((UNITS,)),
        ],
        compiler_params=pltpu.CompilerParams(
            collective_id=0, has_side_effects=True, vmem_limit_bytes=54 * 2**20),
        name="fused",
    )(activations, out_grad, projector, first_moment, second_moment)
    return pl.pallas_call(
        decode,
        out_shape=(
            jax.ShapeDtypeStruct((rows * 8, ff), f32),
            jax.ShapeDtypeStruct(first_moment.shape, f32),
            jax.ShapeDtypeStruct(second_moment.shape, f32),
        ),
        in_specs=[vmem] * 4,
        out_specs=(any_, any_, any_),
        scratch_shapes=[
            pltpu.VMEM((SLOTS, rows * 8, cols), f32),
            dma((SLOTS,)), dma((2,)),
        ],
        compiler_params=pltpu.CompilerParams(vmem_limit_bytes=16 * 2**20),
        name="decode",
    )(basis, norm, nf, ns)


def solution(mesh):
    in_specs = (
        P("dp", None),
        P("dp", "tensor"),
        P(("dp", "tensor"), None),
        P("dp", "tensor"),
        P("dp", "tensor"),
    )
    out_specs = (P("dp", "tensor"), P("dp", "tensor"), P("dp", "tensor"))
    return jax.shard_map(
        per_device, mesh=mesh, in_specs=in_specs, out_specs=out_specs, check_vma=False
    )
```

```python
import jax
import jax.numpy as jnp
from jax import lax
from jax.experimental import pallas as pl
from jax.experimental.pallas import tpu as pltpu
from jax.sharding import PartitionSpec as P

beta_one = 0.9
beta_two = 0.999
bias_one = 1.0 - 0.9**10
bias_two = 1.0 - 0.999**10
adam_eps = 1e-08

MESH = pl.DeviceIdType.MESH
CHUNKS = 7
CHIP_ORDER = (1, 3, 4, 5, 7, 2, 6)
TENSOR_ORDER = (5, 3, 7, 4, 2, 6, 1)
Z_ORDER = (1, 2, 3)
UNITS = 2 * CHUNKS
STEP = 256
LAGS = (2, 1, 0, 7, 13)
SLOTS = 3
NT = (((1,), (1,)), ((), ()))


def fused(act_hbm, grad_hbm, proj_hbm, first_hbm, second_hbm,
          norm, basis, nfirst, nsecond,
          act, grad, proj, part, first, second, slices, acc, pj, res, th_in, out1, in1, out2, in2, total_sent,
          act_sem, grad_sem, local_sem, sent_sem, once_sem,
          b_r, f_r, c_r, t_r, p_r, q_r, g_r, h_r):
    dp = lax.axis_index("dp")
    tn = lax.axis_index("tensor")
    chip, core = dp // 2, dp % 2
    yh, zz = chip // 4, chip % 4
    rows = proj.shape[0]
    width = act.shape[2]
    cols = grad.shape[2]
    own = first.shape[0] // 2

    def chip_to(i):
        return ((yh + i // 4) % 2) * 4 + (zz + i % 4) % 4

    def chip_from(i):
        return ((yh + i // 4) % 2) * 4 + (zz + 4 - i % 4) % 4

    def tensor_to(i):
        return ((tn // 2 + i // 2) % 4) * 2 + (tn % 2 + i % 2) % 2

    def tensor_from(i):
        return ((tn // 2 + 4 - i // 2) % 4) * 2 + (tn % 2 + i % 2) % 2

    def at_chip(i):
        return {"dp": chip_to(i) * 2 + core}

    partner = {"dp": chip * 2 + (1 - core)}

    def remote(src, dst, send, recv, to):
        return pltpu.make_async_remote_copy(src, dst, send, recv, device_id=to, device_id_type=MESH)

    def arrive(ref, sem):
        pltpu.make_async_copy(ref, ref, sem).wait()

    a_s, b_s, f_s, c_s, e_s, t_s, p_s, d_s = (sent_sem.at[i] for i in range(8))
    a_r, e_r, n_s, n_r, d_r = (once_sem.at[i] for i in range(5))

    def act_copy(k):
        return pltpu.make_async_copy(
            act_hbm.at[:, pl.ds(pl.multiple_of(k * width, 128), width)], act.at[k], act_sem.at[k])

    def grad_copy(j):
        return pltpu.make_async_copy(
            grad_hbm.at[:, pl.ds(pl.multiple_of(j * cols, 128), cols)], grad.at[j], grad_sem)

    barrier = pltpu.get_barrier_semaphore()
    for i, k in zip(CHIP_ORDER, TENSOR_ORDER):
        pl.semaphore_signal(barrier, inc=1, device_id=at_chip(i), device_id_type=MESH)
        pl.semaphore_signal(barrier, inc=1, device_id={"tensor": tensor_to(k)}, device_id_type=MESH)
    pl.semaphore_signal(barrier, inc=1, device_id=partner, device_id_type=MESH)

    proj_copy = pltpu.make_async_copy(proj_hbm, proj, local_sem.at[0])
    first_copy = pltpu.make_async_copy(first_hbm, first, local_sem.at[1])
    second_copy = pltpu.make_async_copy(second_hbm, second, local_sem.at[2])
    proj_copy.start()
    my_rows = pl.ds(pl.multiple_of(tn * rows, 16), rows)
    proj_copy.wait()
    for c in (core, 1 - core):
        act_copy(chip * 2 + c).start()
    for i in CHIP_ORDER:
        for c in (core, 1 - core):
            act_copy(chip_from(i) * 2 + c).start()
    for j in range(CHUNKS):
        grad_copy(j).start()
    first_copy.start()
    second_copy.start()

    with jax.named_scope("barrier_wait"):
        pl.semaphore_wait(barrier, 15)

    def lanes(t):
        return pl.ds(pl.multiple_of((t // 2) * 128, 128), 128)

    def a_copy(i):
        return remote(proj.at[:, lanes(tensor_to(i))], part.at[my_rows], a_s, a_r,
                      {"tensor": tensor_to(i)})

    e_near = remote(proj, basis.at[my_rows], n_s, n_r, {"tensor": tensor_to(1)})

    def e_copy(i, x):
        there = pl.ds(pl.multiple_of(x * 2 * rows, 16), 2 * rows)
        return remote(basis.at[there], basis.at[there], e_s, e_r, {"tensor": tensor_to(2 * i)})

    for i in TENSOR_ORDER:
        a_copy(i).start()
    e_near.start()
    part[my_rows] = proj[:, lanes(tn)]
    basis[my_rows] = proj[...]
    ranks = 2 * slices.shape[2]
    row = lax.broadcasted_iota(jnp.int32, (2, 2, own, 128), 2)
    row += own * (lax.broadcasted_iota(jnp.int32, (2, 2, own, 128), 0)
                  + 2 * lax.broadcasted_iota(jnp.int32, (2, 2, own, 128), 1))
    pick = lax.broadcasted_iota(jnp.int32, (2, 2, own, 128), 3) == row + (tn % 2) * ranks
    pick = jnp.where(pick, 1.0, 0.0).reshape(ranks, 128).astype(jnp.bfloat16)
    with jax.named_scope("a_wait"):
        arrive(part.at[0:7 * rows], a_r)

    both = lax.dot_general(pick, part[...], NT, preferred_element_type=jnp.float32).astype(jnp.bfloat16)
    for u in range(2):
        slices[u, dp] = both[u * ranks // 2:(u + 1) * ranks // 2]

    def b_copy(u, i):
        to = at_chip(i) if i else partner
        return remote(slices.at[u, dp], slices.at[u, dp], b_s, b_r.at[u, i], to)

    def f_copy(u, i):
        src = chip_from(i) * 2 + core
        return remote(slices.at[u, src], slices.at[u, src], f_s, f_r.at[u, i], partner)

    for u in range(2):
        for i in CHIP_ORDER + (0,):
            b_copy(u, i).start()

    def project_half(u):
        def product(k):
            if u == 0:
                act_copy(k).wait()
            return lax.dot_general(slices[u, k], act[k], NT, preferred_element_type=jnp.float32)

        with jax.named_scope("near"):
            acc[...] = product(dp)
            b_copy(u, 0).wait_recv()
            acc[...] += product(chip * 2 + (1 - core))

        with jax.named_scope("arrived"):
            for i, before in zip(CHIP_ORDER + (None,), (None,) + CHIP_ORDER):
                if i is not None:
                    b_copy(u, i).wait_recv()
                    f_copy(u, i).start()
                    acc[...] += product(chip_from(i) * 2 + core)
                if before is not None:
                    f_copy(u, before).wait_recv()
                    acc[...] += product(chip_from(before) * 2 + (1 - core))

    def block(t):
        return pl.ds(pl.multiple_of(t * own, 16), own)

    def c_copy(u, side, i, k):
        return remote(pj.at[u, side, block(tn)], pj.at[u, side, block(tn)], c_s, c_r.at[k],
                      {"tensor": tensor_to(i)})

    def c_wait(k):
        with jax.named_scope("c_wait"):
            arrive(pj.at[0, 0, 0:7 * own], c_r.at[k])

    for u in range(2):
        project_half(u)
        done = acc[...].astype(jnp.bfloat16)
        for c in range(2):
            pj[u, c, block(tn)] = done[c * own:(c + 1) * own]
        for k in (2 * u, 2 * u + 1):
            for i in range(1, 8):
                c_copy(u, (core + 1 + k) % 2, i, k).start()
    arrive(grad, grad_sem)
    e_near.wait_recv()
    for i in Z_ORDER:
        e_copy(i, tn // 2).start()

    def t_copy(n):
        return remote(res.at[n, 1 - core], th_in.at[n], t_s, t_r.at[n], partner)

    def half_dots(n, side):
        for s in range(0, cols, STEP):
            w = min(STEP, cols - s)
            res[n, side, :, :, :, s:s + w] = jnp.dot(
                pj[n // CHUNKS, side], grad[n % CHUNKS, :, s:s + w], preferred_element_type=jnp.float32
            ).reshape(2, 4, own, w)

    def theirs(n):
        half_dots(n, 1 - core)
        t_copy(n).start()

    def mine(n):
        half_dots(n, core)

    def p_y(j):
        return remote(out1.at[j, 1 - yh], in1.at[j, :, 0], p_s, p_r.at[j], at_chip(4))

    def p_z(j, i):
        return remote(out1.at[j, :, (zz + i) % 4], in1.at[j, i], p_s, p_r.at[j], at_chip(i))

    def q_z(j, i):
        return remote(out2.at[j, (zz + i) % 4], in2.at[j, i], p_s, q_r.at[j], at_chip(i))

    def q_y(j):
        return remote(out2.at[j, 1 - yh], in2.at[j, 0], p_s, q_r.at[j], at_chip(4))

    def g_z(j, i, z):
        return remote(norm.at[j, core, yh, z], norm.at[j, core, yh, z], p_s, g_r.at[j], at_chip(i))

    def g_y(j, y):
        return remote(norm.at[j, core, y, zz], norm.at[j, core, y, zz], p_s, g_r.at[j], at_chip(4))

    def h_y(j, y):
        return remote(norm.at[j, core, y], norm.at[j, core, y], p_s, h_r.at[j], at_chip(4))

    def h_z(j, i, z):
        return remote(norm.at[j, core, :, z], norm.at[j, core, :, z], p_s, h_r.at[j], at_chip(i))

    def d_copy(j, c):
        return remote(norm.at[j, c], norm.at[j, c], d_s, d_r, partner)

    def reduce_z(n):
        return n % 2 == 0

    def gather_y(n):
        return n % 2 == 1

    def y_first(n):
        return pl.when(jnp.logical_not(reduce_z(n)))

    def z_first(n):
        return pl.when(reduce_z(n))

    def then_y(n):
        return pl.when(jnp.logical_not(gather_y(n)))

    def then_z(n):
        return pl.when(gather_y(n))

    def combine(n):
        t_copy(n).wait_recv()

        @y_first(n)
        def _():
            out1[n, 1 - yh] = (res[n, core, 1 - yh] + th_in[n, 1 - yh]).astype(jnp.bfloat16)
            p_y(n).start()

        @z_first(n)
        def _():
            for i in Z_ORDER:
                z = (zz + i) % 4
                out1[n, :, z] = (res[n, core, :, z] + th_in[n, :, z]).astype(jnp.bfloat16)
                p_z(n, i).start()

    def stage_one(j):
        @y_first(j)
        def _():
            p_y(j).wait_recv()
            total = res[j, core, yh] + th_in[j, yh] + in1[j, :, 0].astype(jnp.float32)
            res[j, core, yh] = total
            out2[j] = total.astype(jnp.bfloat16)
            for i in Z_ORDER:
                q_z(j, i).start()

        @z_first(j)
        def _():
            total = res[j, core, :, zz] + th_in[j, :, zz]
            arrive(in1.at[j, 1:4], p_r.at[j])
            for i in range(1, 4):
                total += in1[j, i].astype(jnp.float32)
            res[j, core, :, zz] = total
            out2[j, 0:2] = total.astype(jnp.bfloat16)
            q_y(j).start()

    def adam(j):
        @y_first(j)
        def _():
            total = res[j, core, yh, zz]
            arrive(in2.at[j, 1:4], q_r.at[j])
            for i in range(1, 4):
                total += in2[j, i].astype(jnp.float32)
            res[j, core, yh, zz] = total

        @z_first(j)
        def _():
            q_y(j).wait_recv()
            res[j, core, yh, zz] = res[j, core, yh, zz] + in2[j, 0].astype(jnp.float32)

        total = res[j, core, yh, zz]
        at = (pl.ds(pl.multiple_of((j // CHUNKS) * own, 8), own),
              pl.ds(pl.multiple_of((j % CHUNKS) * cols, 128), cols))
        new_first = beta_one * first[at] + (1.0 - beta_one) * total
        new_second = beta_two * second[at] + (1.0 - beta_two) * total * total
        nfirst[at] = new_first
        nsecond[at] = new_second
        norm[j, core, yh, zz] = (
            new_first / bias_one / (jnp.sqrt(new_second / bias_two) + adam_eps)).astype(jnp.bfloat16)

        @then_y(j)
        def _():
            for i in Z_ORDER:
                g_z(j, i, zz).start()

        @then_z(j)
        def _():
            g_y(j, yh).start()

    def stage_two(j):
        @then_y(j)
        def _():
            arrive(norm.at[j, core, yh, 0:3], g_r.at[j])
            h_y(j, yh).start()

        @then_z(j)
        def _():
            g_y(j, 1 - yh).wait_recv()
            for i in Z_ORDER:
                h_z(j, i, zz).start()

    def to_pair(j):
        @then_y(j)
        def _():
            h_y(j, 1 - yh).wait_recv()

        @then_z(j)
        def _():
            arrive(norm.at[j, core, :, 0:3], h_r.at[j])

        d_copy(j, core).start()

    def loop(steps, *stages):
        def body(k, _):
            for name, do, lag, first_unit, count in stages:
                @pl.when(jnp.logical_and(k >= lag, k < lag + count))
                def _():
                    with jax.named_scope(name):
                        do(first_unit + k - lag)
            return 0

        lax.fori_loop(0, steps, body, 0)

    c_wait(0)
    loop(CHUNKS, ("theirs", theirs, 0, 0, CHUNKS))
    c_wait(1)
    loop(CHUNKS, ("dots", mine, 0, 0, CHUNKS), ("combine", combine, 0, 0, CHUNKS))
    c_wait(2)
    loop(CHUNKS, ("theirs", theirs, 0, CHUNKS, CHUNKS))
    c_wait(3)
    loop(CHUNKS + LAGS[1], ("dots", mine, 0, CHUNKS, CHUNKS), ("combine", combine, 0, CHUNKS, CHUNKS),
         ("one", stage_one, LAGS[1], 0, CHUNKS))
    first_copy.wait()
    second_copy.wait()
    loop(UNITS + LAGS[4], ("one", stage_one, 0, CHUNKS, CHUNKS), ("adam", adam, LAGS[2], 0, UNITS),
         ("two", stage_two, LAGS[3], 0, UNITS), ("pair", to_pair, LAGS[4], 0, UNITS))

    with jax.named_scope("finish"):
        arrive(part.at[0:7 * rows], a_s)
        arrive(slices.at[0], b_s)
        arrive(slices.at[0, 0:14], f_s)
        arrive(pj.at[:, :, 0:7 * own], c_s)
        e_near.wait_send()
        arrive(basis.at[0:6 * rows], e_s)
        arrive(basis.at[0:6 * rows], e_r)
        arrive(res.at[:, 0], t_s)
        arrive(total_sent, p_s)
        arrive(norm.at[:, 0], d_s)
        arrive(norm.at[:, 0], d_r)


def decode(basis, norm, nf, ns, update, nf_out, ns_out, buf, sem, small_sem):
    cols = norm.shape[5]
    nf_copy = pltpu.make_async_copy(nf, nf_out, small_sem.at[0])
    ns_copy = pltpu.make_async_copy(ns, ns_out, small_sem.at[1])

    def out_copy(j):
        return pltpu.make_async_copy(
            buf.at[j % SLOTS], update.at[:, pl.ds(pl.multiple_of(j * cols, 128), cols)], sem.at[j % SLOTS])

    def step(j, _):
        @pl.when(j >= SLOTS)
        def _():
            out_copy(j - SLOTS).wait()
        block = jnp.concatenate(
            [norm[u * CHUNKS + j, c, y, z]
             for y in range(2) for z in range(4) for c in range(2) for u in range(2)], axis=0)
        buf[j % SLOTS] = jnp.dot(basis[...], block, preferred_element_type=jnp.float32)
        out_copy(j).start()
        return 0

    lax.fori_loop(0, CHUNKS, step, 0)
    nf_copy.start()
    ns_copy.start()
    for j in range(CHUNKS - SLOTS, CHUNKS):
        out_copy(j).wait()
    nf_copy.wait()
    ns_copy.wait()


def per_device(activations, out_grad, projector, first_moment, second_moment):
    tokens, width = activations.shape
    ff = out_grad.shape[1]
    rows, rank = projector.shape
    own = first_moment.shape[0] // 2
    cols = ff // CHUNKS
    half = rank // 2
    bf, f32 = jnp.bfloat16, jnp.float32
    vmem = pl.BlockSpec(memory_space=pltpu.VMEM)
    any_ = pl.BlockSpec(memory_space=pl.ANY)
    dma = pltpu.SemaphoreType.DMA
    norm, basis, nf, ns = pl.pallas_call(
        fused,
        out_shape=(
            pltpu.VMEM((UNITS, 2, 2, 4, own, cols), bf),
            pltpu.VMEM((rows * 8, rank), bf),
            pltpu.VMEM(first_moment.shape, f32),
            pltpu.VMEM(second_moment.shape, f32),
        ),
        in_specs=[any_] * 5,
        out_specs=(vmem, vmem, vmem, vmem),
        scratch_shapes=[
            pltpu.VMEM((16, tokens, width // 16), bf),
            pltpu.VMEM((CHUNKS, tokens, cols), bf),
            pltpu.VMEM((rows, rank), bf),
            pltpu.VMEM((rows * 8, 128), bf),
            pltpu.VMEM(first_moment.shape, f32),
            pltpu.VMEM(second_moment.shape, f32),
            pltpu.VMEM((2, 16, rank // 16, width // 16), bf),
            pltpu.VMEM((rank // 16, tokens), f32),
            pltpu.VMEM((2, 2, half // 2, tokens), bf),
            pltpu.VMEM((UNITS, 2, 2, 4, own, cols), f32),
            pltpu.VMEM((UNITS, 2, 4, own, cols), f32),
            pltpu.VMEM((UNITS, 2, 4, own, cols), bf),
            pltpu.VMEM((UNITS, 4, 2, own, cols), bf),
            pltpu.VMEM((UNITS, 4, own, cols), bf),
            pltpu.VMEM((UNITS, 4, own, cols), bf),
            pltpu.VMEM((UNITS, 14, own, cols), bf),
            dma((16,)), dma, dma((3,)), dma((8,)), dma((5,)),
            dma((2, 8)), dma((2, 8)), dma((4,)), dma((UNITS,)),
            dma((UNITS,)), dma((UNITS,)), dma((UNITS,)), dma((UNITS,)),
        ],
        compiler_params=pltpu.CompilerParams(
            collective_id=0, has_side_effects=True, vmem_limit_bytes=54 * 2**20),
        name="fused",
    )(activations, out_grad, projector, first_moment, second_moment)
    return pl.pallas_call(
        decode,
        out_shape=(
            jax.ShapeDtypeStruct((rows * 8, ff), f32),
            jax.ShapeDtypeStruct(first_moment.shape, f32),
            jax.ShapeDtypeStruct(second_moment.shape, f32),
        ),
        in_specs=[vmem] * 4,
        out_specs=(any_, any_, any_),
        scratch_shapes=[
            pltpu.VMEM((SLOTS, rows * 8, cols), f32),
            dma((SLOTS,)), dma((2,)),
        ],
        compiler_params=pltpu.CompilerParams(vmem_limit_bytes=16 * 2**20),
        name="decode",
    )(basis, norm, nf, ns)


def solution(mesh):
    in_specs = (
        P("dp", None),
        P("dp", "tensor"),
        P(("dp", "tensor"), None),
        P("dp", "tensor"),
        P("dp", "tensor"),
    )
    out_specs = (P("dp", "tensor"), P("dp", "tensor"), P("dp", "tensor"))
    return jax.shard_map(
        per_device, mesh=mesh, in_specs=in_specs, out_specs=out_specs, check_vma=False
    )
```

```python
import jax
import jax.numpy as jnp
from jax import lax
from jax.experimental import pallas as pl
from jax.experimental.pallas import tpu as pltpu
from jax.sharding import PartitionSpec as P

beta_one = 0.9
beta_two = 0.999
bias_one = 1.0 - 0.9**10
bias_two = 1.0 - 0.999**10
adam_eps = 1e-08

MESH = pl.DeviceIdType.MESH
CHUNKS = 7
CHIP_ORDER = (1, 3, 4, 5, 7, 2, 6)
TENSOR_ORDER = (5, 3, 7, 4, 2, 6, 1)
Z_ORDER = (1, 2, 3)
UNITS = 2 * CHUNKS
STEP = 256
LAGS = (2, 1, 0, 7, 13)
SLOTS = 4
NT = (((1,), (1,)), ((), ()))


def fused(act_hbm, grad_hbm, proj_hbm, first_hbm, second_hbm,
          norm, basis, nfirst, nsecond,
          act, grad, proj, part, first, second, slices, acc, pj, res, th_in, out1, in1, out2, in2, total_sent,
          act_sem, grad_sem, local_sem, sent_sem, once_sem,
          b_r, f_r, c_r, t_r, p_r, q_r, g_r, h_r):
    dp = lax.axis_index("dp")
    tn = lax.axis_index("tensor")
    chip, core = dp // 2, dp % 2
    yh, zz = chip // 4, chip % 4
    rows = proj.shape[0]
    width = act.shape[2]
    cols = grad.shape[2]
    own = first.shape[0] // 2

    def chip_to(i):
        return ((yh + i // 4) % 2) * 4 + (zz + i % 4) % 4

    def chip_from(i):
        return ((yh + i // 4) % 2) * 4 + (zz + 4 - i % 4) % 4

    def tensor_to(i):
        return ((tn // 2 + i // 2) % 4) * 2 + (tn % 2 + i % 2) % 2

    def tensor_from(i):
        return ((tn // 2 + 4 - i // 2) % 4) * 2 + (tn % 2 + i % 2) % 2

    def at_chip(i):
        return {"dp": chip_to(i) * 2 + core}

    partner = {"dp": chip * 2 + (1 - core)}

    def remote(src, dst, send, recv, to):
        return pltpu.make_async_remote_copy(src, dst, send, recv, device_id=to, device_id_type=MESH)

    def arrive(ref, sem):
        pltpu.make_async_copy(ref, ref, sem).wait()

    a_s, b_s, f_s, c_s, e_s, t_s, p_s, d_s = (sent_sem.at[i] for i in range(8))
    a_r, e_r, n_s, n_r, d_r = (once_sem.at[i] for i in range(5))

    def act_copy(k):
        return pltpu.make_async_copy(
            act_hbm.at[:, pl.ds(pl.multiple_of(k * width, 128), width)], act.at[k], act_sem.at[k])

    def grad_copy(j):
        return pltpu.make_async_copy(
            grad_hbm.at[:, pl.ds(pl.multiple_of(j * cols, 128), cols)], grad.at[j], grad_sem)

    barrier = pltpu.get_barrier_semaphore()
    for i, k in zip(CHIP_ORDER, TENSOR_ORDER):
        pl.semaphore_signal(barrier, inc=1, device_id=at_chip(i), device_id_type=MESH)
        pl.semaphore_signal(barrier, inc=1, device_id={"tensor": tensor_to(k)}, device_id_type=MESH)
    pl.semaphore_signal(barrier, inc=1, device_id=partner, device_id_type=MESH)

    proj_copy = pltpu.make_async_copy(proj_hbm, proj, local_sem.at[0])
    first_copy = pltpu.make_async_copy(first_hbm, first, local_sem.at[1])
    second_copy = pltpu.make_async_copy(second_hbm, second, local_sem.at[2])
    proj_copy.start()
    my_rows = pl.ds(pl.multiple_of(tn * rows, 16), rows)
    proj_copy.wait()
    for c in (core, 1 - core):
        act_copy(chip * 2 + c).start()
    for i in CHIP_ORDER:
        for c in (core, 1 - core):
            act_copy(chip_from(i) * 2 + c).start()
    for j in range(CHUNKS):
        grad_copy(j).start()
    first_copy.start()
    second_copy.start()

    with jax.named_scope("barrier_wait"):
        pl.semaphore_wait(barrier, 15)

    def lanes(t):
        return pl.ds(pl.multiple_of((t // 2) * 128, 128), 128)

    def a_copy(i):
        return remote(proj.at[:, lanes(tensor_to(i))], part.at[my_rows], a_s, a_r,
                      {"tensor": tensor_to(i)})

    e_near = remote(proj, basis.at[my_rows], n_s, n_r, {"tensor": tensor_to(1)})

    def e_copy(i, x):
        there = pl.ds(pl.multiple_of(x * 2 * rows, 16), 2 * rows)
        return remote(basis.at[there], basis.at[there], e_s, e_r, {"tensor": tensor_to(2 * i)})

    for i in TENSOR_ORDER:
        a_copy(i).start()
    e_near.start()
    part[my_rows] = proj[:, lanes(tn)]
    basis[my_rows] = proj[...]
    ranks = 2 * slices.shape[2]
    row = lax.broadcasted_iota(jnp.int32, (2, 2, own, 128), 2)
    row += own * (lax.broadcasted_iota(jnp.int32, (2, 2, own, 128), 0)
                  + 2 * lax.broadcasted_iota(jnp.int32, (2, 2, own, 128), 1))
    pick = lax.broadcasted_iota(jnp.int32, (2, 2, own, 128), 3) == row + (tn % 2) * ranks
    pick = jnp.where(pick, 1.0, 0.0).reshape(ranks, 128).astype(jnp.bfloat16)
    with jax.named_scope("a_wait"):
        arrive(part.at[0:7 * rows], a_r)

    both = lax.dot_general(pick, part[...], NT, preferred_element_type=jnp.float32).astype(jnp.bfloat16)
    for u in range(2):
        slices[u, dp] = both[u * ranks // 2:(u + 1) * ranks // 2]

    def b_copy(u, i):
        to = at_chip(i) if i else partner
        return remote(slices.at[u, dp], slices.at[u, dp], b_s, b_r.at[u, i], to)

    def f_copy(u, i):
        src = chip_from(i) * 2 + core
        return remote(slices.at[u, src], slices.at[u, src], f_s, f_r.at[u, i], partner)

    for u in range(2):
        for i in CHIP_ORDER + (0,):
            b_copy(u, i).start()

    def project_half(u):
        def product(k):
            if u == 0:
                act_copy(k).wait()
            return lax.dot_general(slices[u, k], act[k], NT, preferred_element_type=jnp.float32)

        with jax.named_scope("near"):
            acc[...] = product(dp)
            b_copy(u, 0).wait_recv()
            acc[...] += product(chip * 2 + (1 - core))

        with jax.named_scope("arrived"):
            for i, before in zip(CHIP_ORDER + (None,), (None,) + CHIP_ORDER):
                if i is not None:
                    b_copy(u, i).wait_recv()
                    f_copy(u, i).start()
                    acc[...] += product(chip_from(i) * 2 + core)
                if before is not None:
                    f_copy(u, before).wait_recv()
                    acc[...] += product(chip_from(before) * 2 + (1 - core))

    def block(t):
        return pl.ds(pl.multiple_of(t * own, 16), own)

    def c_copy(u, side, i, k):
        return remote(pj.at[u, side, block(tn)], pj.at[u, side, block(tn)], c_s, c_r.at[k],
                      {"tensor": tensor_to(i)})

    def c_wait(k):
        with jax.named_scope("c_wait"):
            arrive(pj.at[0, 0, 0:7 * own], c_r.at[k])

    for u in range(2):
        project_half(u)
        done = acc[...].astype(jnp.bfloat16)
        for c in range(2):
            pj[u, c, block(tn)] = done[c * own:(c + 1) * own]
        for k in (2 * u, 2 * u + 1):
            for i in range(1, 8):
                c_copy(u, (core + 1 + k) % 2, i, k).start()
    arrive(grad, grad_sem)
    e_near.wait_recv()
    for i in Z_ORDER:
        e_copy(i, tn // 2).start()

    def t_copy(n):
        return remote(res.at[n, 1 - core], th_in.at[n], t_s, t_r.at[n], partner)

    def half_dots(n, side):
        for s in range(0, cols, STEP):
            w = min(STEP, cols - s)
            res[n, side, :, :, :, s:s + w] = jnp.dot(
                pj[n // CHUNKS, side], grad[n % CHUNKS, :, s:s + w], preferred_element_type=jnp.float32
            ).reshape(2, 4, own, w)

    def theirs(n):
        half_dots(n, 1 - core)
        t_copy(n).start()

    def mine(n):
        half_dots(n, core)

    def p_y(j):
        return remote(out1.at[j, 1 - yh], in1.at[j, :, 0], p_s, p_r.at[j], at_chip(4))

    def p_z(j, i):
        return remote(out1.at[j, :, (zz + i) % 4], in1.at[j, i], p_s, p_r.at[j], at_chip(i))

    def q_z(j, i):
        return remote(out2.at[j, (zz + i) % 4], in2.at[j, i], p_s, q_r.at[j], at_chip(i))

    def q_y(j):
        return remote(out2.at[j, 1 - yh], in2.at[j, 0], p_s, q_r.at[j], at_chip(4))

    def g_z(j, i, z):
        return remote(norm.at[j, core, yh, z], norm.at[j, core, yh, z], p_s, g_r.at[j], at_chip(i))

    def g_y(j, y):
        return remote(norm.at[j, core, y, zz], norm.at[j, core, y, zz], p_s, g_r.at[j], at_chip(4))

    def h_y(j, y):
        return remote(norm.at[j, core, y], norm.at[j, core, y], p_s, h_r.at[j], at_chip(4))

    def h_z(j, i, z):
        return remote(norm.at[j, core, :, z], norm.at[j, core, :, z], p_s, h_r.at[j], at_chip(i))

    def d_copy(j, c):
        return remote(norm.at[j, c], norm.at[j, c], d_s, d_r, partner)

    def reduce_z(n):
        return n % 2 == 0

    def gather_y(n):
        return n % 2 == 1

    def y_first(n):
        return pl.when(jnp.logical_not(reduce_z(n)))

    def z_first(n):
        return pl.when(reduce_z(n))

    def then_y(n):
        return pl.when(jnp.logical_not(gather_y(n)))

    def then_z(n):
        return pl.when(gather_y(n))

    def combine(n):
        t_copy(n).wait_recv()

        @y_first(n)
        def _():
            out1[n, 1 - yh] = (res[n, core, 1 - yh] + th_in[n, 1 - yh]).astype(jnp.bfloat16)
            p_y(n).start()

        @z_first(n)
        def _():
            for i in Z_ORDER:
                z = (zz + i) % 4
                out1[n, :, z] = (res[n, core, :, z] + th_in[n, :, z]).astype(jnp.bfloat16)
                p_z(n, i).start()

    def stage_one(j):
        @y_first(j)
        def _():
            p_y(j).wait_recv()
            total = res[j, core, yh] + th_in[j, yh] + in1[j, :, 0].astype(jnp.float32)
            res[j, core, yh] = total
            out2[j] = total.astype(jnp.bfloat16)
            for i in Z_ORDER:
                q_z(j, i).start()

        @z_first(j)
        def _():
            total = res[j, core, :, zz] + th_in[j, :, zz]
            arrive(in1.at[j, 1:4], p_r.at[j])
            for i in range(1, 4):
                total += in1[j, i].astype(jnp.float32)
            res[j, core, :, zz] = total
            out2[j, 0:2] = total.astype(jnp.bfloat16)
            q_y(j).start()

    def adam(j):
        @y_first(j)
        def _():
            total = res[j, core, yh, zz]
            arrive(in2.at[j, 1:4], q_r.at[j])
            for i in range(1, 4):
                total += in2[j, i].astype(jnp.float32)
            res[j, core, yh, zz] = total

        @z_first(j)
        def _():
            q_y(j).wait_recv()
            res[j, core, yh, zz] = res[j, core, yh, zz] + in2[j, 0].astype(jnp.float32)

        total = res[j, core, yh, zz]
        at = (pl.ds(pl.multiple_of((j // CHUNKS) * own, 8), own),
              pl.ds(pl.multiple_of((j % CHUNKS) * cols, 128), cols))
        new_first = beta_one * first[at] + (1.0 - beta_one) * total
        new_second = beta_two * second[at] + (1.0 - beta_two) * total * total
        nfirst[at] = new_first
        nsecond[at] = new_second
        norm[j, core, yh, zz] = (
            new_first / bias_one / (jnp.sqrt(new_second / bias_two) + adam_eps)).astype(jnp.bfloat16)

        @then_y(j)
        def _():
            for i in Z_ORDER:
                g_z(j, i, zz).start()

        @then_z(j)
        def _():
            g_y(j, yh).start()

    def stage_two(j):
        @then_y(j)
        def _():
            arrive(norm.at[j, core, yh, 0:3], g_r.at[j])
            h_y(j, yh).start()

        @then_z(j)
        def _():
            g_y(j, 1 - yh).wait_recv()
            for i in Z_ORDER:
                h_z(j, i, zz).start()

    def to_pair(j):
        @then_y(j)
        def _():
            h_y(j, 1 - yh).wait_recv()

        @then_z(j)
        def _():
            arrive(norm.at[j, core, :, 0:3], h_r.at[j])

        d_copy(j, core).start()

    def loop(steps, *stages):
        def body(k, _):
            for name, do, lag, first_unit, count in stages:
                @pl.when(jnp.logical_and(k >= lag, k < lag + count))
                def _():
                    with jax.named_scope(name):
                        do(first_unit + k - lag)
            return 0

        lax.fori_loop(0, steps, body, 0)

    c_wait(0)
    loop(CHUNKS, ("theirs", theirs, 0, 0, CHUNKS))
    c_wait(1)
    loop(CHUNKS, ("dots", mine, 0, 0, CHUNKS), ("combine", combine, 0, 0, CHUNKS))
    c_wait(2)
    loop(CHUNKS, ("theirs", theirs, 0, CHUNKS, CHUNKS))
    c_wait(3)
    loop(CHUNKS + LAGS[1], ("dots", mine, 0, CHUNKS, CHUNKS), ("combine", combine, 0, CHUNKS, CHUNKS),
         ("one", stage_one, LAGS[1], 0, CHUNKS))
    first_copy.wait()
    second_copy.wait()
    loop(UNITS + LAGS[4], ("one", stage_one, 0, CHUNKS, CHUNKS), ("adam", adam, LAGS[2], 0, UNITS),
         ("two", stage_two, LAGS[3], 0, UNITS), ("pair", to_pair, LAGS[4], 0, UNITS))

    with jax.named_scope("finish"):
        arrive(part.at[0:7 * rows], a_s)
        arrive(slices.at[0], b_s)
        arrive(slices.at[0, 0:14], f_s)
        arrive(pj.at[:, :, 0:7 * own], c_s)
        e_near.wait_send()
        arrive(basis.at[0:6 * rows], e_s)
        arrive(basis.at[0:6 * rows], e_r)
        arrive(res.at[:, 0], t_s)
        arrive(total_sent, p_s)
        arrive(norm.at[:, 0], d_s)
        arrive(norm.at[:, 0], d_r)


def decode(basis, norm, nf, ns, update, nf_out, ns_out, buf, sem, small_sem):
    cols = norm.shape[5]
    nf_copy = pltpu.make_async_copy(nf, nf_out, small_sem.at[0])
    ns_copy = pltpu.make_async_copy(ns, ns_out, small_sem.at[1])

    def out_copy(j):
        return pltpu.make_async_copy(
            buf.at[j % SLOTS], update.at[:, pl.ds(pl.multiple_of(j * cols, 128), cols)], sem.at[j % SLOTS])

    def step(j, _):
        @pl.when(j >= SLOTS)
        def _():
            out_copy(j - SLOTS).wait()
        block = jnp.concatenate(
            [norm[u * CHUNKS + j, c, y, z]
             for y in range(2) for z in range(4) for c in range(2) for u in range(2)], axis=0)
        buf[j % SLOTS] = jnp.dot(basis[...], block, preferred_element_type=jnp.float32)
        out_copy(j).start()
        return 0

    nf_copy.start()
    ns_copy.start()
    lax.fori_loop(0, CHUNKS, step, 0)
    for j in range(CHUNKS - SLOTS, CHUNKS):
        out_copy(j).wait()
    nf_copy.wait()
    ns_copy.wait()


def per_device(activations, out_grad, projector, first_moment, second_moment):
    tokens, width = activations.shape
    ff = out_grad.shape[1]
    rows, rank = projector.shape
    own = first_moment.shape[0] // 2
    cols = ff // CHUNKS
    half = rank // 2
    bf, f32 = jnp.bfloat16, jnp.float32
    vmem = pl.BlockSpec(memory_space=pltpu.VMEM)
    any_ = pl.BlockSpec(memory_space=pl.ANY)
    dma = pltpu.SemaphoreType.DMA
    norm, basis, nf, ns = pl.pallas_call(
        fused,
        out_shape=(
            pltpu.VMEM((UNITS, 2, 2, 4, own, cols), bf),
            pltpu.VMEM((rows * 8, rank), bf),
            pltpu.VMEM(first_moment.shape, f32),
            pltpu.VMEM(second_moment.shape, f32),
        ),
        in_specs=[any_] * 5,
        out_specs=(vmem, vmem, vmem, vmem),
        scratch_shapes=[
            pltpu.VMEM((16, tokens, width // 16), bf),
            pltpu.VMEM((CHUNKS, tokens, cols), bf),
            pltpu.VMEM((rows, rank), bf),
            pltpu.VMEM((rows * 8, 128), bf),
            pltpu.VMEM(first_moment.shape, f32),
            pltpu.VMEM(second_moment.shape, f32),
            pltpu.VMEM((2, 16, rank // 16, width // 16), bf),
            pltpu.VMEM((rank // 16, tokens), f32),
            pltpu.VMEM((2, 2, half // 2, tokens), bf),
            pltpu.VMEM((UNITS, 2, 2, 4, own, cols), f32),
            pltpu.VMEM((UNITS, 2, 4, own, cols), f32),
            pltpu.VMEM((UNITS, 2, 4, own, cols), bf),
            pltpu.VMEM((UNITS, 4, 2, own, cols), bf),
            pltpu.VMEM((UNITS, 4, own, cols), bf),
            pltpu.VMEM((UNITS, 4, own, cols), bf),
            pltpu.VMEM((UNITS, 14, own, cols), bf),
            dma((16,)), dma, dma((3,)), dma((8,)), dma((5,)),
            dma((2, 8)), dma((2, 8)), dma((4,)), dma((UNITS,)),
            dma((UNITS,)), dma((UNITS,)), dma((UNITS,)), dma((UNITS,)),
        ],
        compiler_params=pltpu.CompilerParams(
            collective_id=0, has_side_effects=True, vmem_limit_bytes=54 * 2**20),
        name="fused",
    )(activations, out_grad, projector, first_moment, second_moment)
    return pl.pallas_call(
        decode,
        out_shape=(
            jax.ShapeDtypeStruct((rows * 8, ff), f32),
            jax.ShapeDtypeStruct(first_moment.shape, f32),
            jax.ShapeDtypeStruct(second_moment.shape, f32),
        ),
        in_specs=[vmem] * 4,
        out_specs=(any_, any_, any_),
        scratch_shapes=[
            pltpu.VMEM((SLOTS, rows * 8, cols), f32),
            dma((SLOTS,)), dma((2,)),
        ],
        compiler_params=pltpu.CompilerParams(vmem_limit_bytes=16 * 2**20),
        name="decode",
    )(basis, norm, nf, ns)


def solution(mesh):
    in_specs = (
        P("dp", None),
        P("dp", "tensor"),
        P(("dp", "tensor"), None),
        P("dp", "tensor"),
        P("dp", "tensor"),
    )
    out_specs = (P("dp", "tensor"), P("dp", "tensor"), P("dp", "tensor"))
    return jax.shard_map(
        per_device, mesh=mesh, in_specs=in_specs, out_specs=out_specs, check_vma=False
    )
```
